32 devices in a mesh: row: 4 (over x, core), col: 8 (over z, y).
Axes of the slice: x: 2, y: 2, z: 4, core: 2. Of those that a mesh axis runs over, the one named last changes fastest.
Arguments:
- gradients: bfloat16 [8, 4, 8, 32, 512], P(None, 'row', 'col'), may hold values from -2.5 to 2.5
- feature_weights: float32 [512], replicated, may hold values from 0.005859375 to 0.029296875
- order: int32 [8, 4, 256], P(None, 'row'), may hold values from 0 to 255, each once within a row
Outputs:
- factored: float32 [8, 4, 4, 8, 256, 256], P(None, 'row', None, 'col')
The draws below stay inside these ranges and needn't reach their ends.
Inputs may be any that keep to these rules, and one draw needn't show every extreme that they name: Each order[a, r, :] is a permutation of 0 to 255.
All inputs are finite; a program needn't handle non-finite values.
Results may differ from the reference program's by a relative error of at most 0.0025.
Values may be sent and summed in bfloat16 or wider, within the bound.
A program may use at most 64 MiB of HBM per device.

```python
import math
import jax
import jax.numpy as jnp
from jax import lax

FEATURES = 512
PANEL = 256
COL_BLOCKS = 4
ROW_BLOCKS = 8
BLOCKS = 32
WINDOW = 8192
SLICE = 32
N_ROW = 4
N_COL = 8


def levels(stream_key, shape, pieces, low, largest):
    def one(axis_at, shards_of):
        draws = jax.random.uniform(jax.random.fold_in(jax.random.fold_in(stream_key, 6), axis_at), (shards_of,), jnp.float32, low / len(pieces), largest / len(pieces))
        return jnp.repeat(jnp.exp(draws), shape[axis_at] // shards_of).reshape((-1,) + (1,) * (len(shape) - axis_at - 1))

    loudness = one(*pieces[0])
    for cut in pieces[1:]:
        loudness = loudness * one(*cut)
    return loudness


def bell_draw(stream_key, extent, spread, limit, pieces=(), held_as=jnp.bfloat16):
    array = spread * jax.random.normal(stream_key, extent, jnp.float32)
    if pieces:
        array = array * levels(stream_key, extent, pieces, -0.22, 0.18)
    return jnp.clip(array, -limit, limit).astype(held_as)


def setup_inputs(seed: int = 0) -> dict:
    keys = jax.random.split(jax.random.key(seed), 4)
    gradients = bell_draw(keys[0], (ROW_BLOCKS, N_ROW, N_COL, SLICE, FEATURES), 0.42, 2.5, ((1, 4), (2, 8)))
    feature_weights = jnp.clip(jnp.exp(jax.random.uniform(keys[1], (FEATURES,), jnp.float32, math.log(0.005859375), math.log(0.029296875))), 0.005859375, 0.029296875)
    order = jax.vmap(lambda own: jax.random.permutation(own, PANEL))(jax.random.split(keys[2], ROW_BLOCKS * N_ROW)).reshape((ROW_BLOCKS, N_ROW, PANEL)).astype(jnp.int32)
    return dict(gradients=gradients, feature_weights=feature_weights, order=order)


RIDGE = 0.5
EXACT = lax.Precision.HIGHEST

def reference(gradients, feature_weights, order):
    stacked = gradients.reshape(ROW_BLOCKS * N_ROW, PANEL, FEATURES)
    slot_ids = order.reshape(ROW_BLOCKS * N_ROW, PANEL)
    candidates = jnp.take_along_axis(stacked, slot_ids[:, :, None], axis=1).reshape(WINDOW, FEATURES)
    widened = candidates.astype(jnp.float32)
    rounded = lax.optimization_barrier((widened * feature_weights).astype(jnp.bfloat16))
    scaled = rounded.astype(jnp.float32)
    squares = jnp.sum(scaled * widened, axis=1)
    positions = jnp.arange(WINDOW, dtype=jnp.int32)

    def block_rows(packed):
        left_side, left_squares, offset = packed
        products = jnp.dot(left_side, widened.T, precision=EXACT)
        strip = jnp.exp(-0.5 * (left_squares[:, None] + squares[None, :] - 2.0 * products))
        diagonal = ((offset + jnp.arange(PANEL, dtype=jnp.int32))[:, None] == positions[None, :]).astype(jnp.float32)
        return strip + RIDGE * diagonal
    offsets = jnp.arange(BLOCKS, dtype=jnp.int32) * PANEL
    matrix = lax.map(block_rows, (scaled.reshape(BLOCKS, PANEL, FEATURES), squares.reshape(BLOCKS, PANEL), offsets))
    matrix = matrix.reshape(WINDOW, WINDOW)
    lower_first = jnp.linalg.cholesky(matrix[:PANEL, :PANEL])
    panel_first = lax.linalg.triangular_solve(lower_first, matrix[:, :PANEL], left_side=False, lower=True, transpose_a=True)
    panel_first = panel_first.at[:PANEL].set(lower_first)
    middle = matrix - jnp.dot(panel_first, panel_first.T, precision=EXACT)
    lower_second = jnp.linalg.cholesky(middle[PANEL:2 * PANEL, PANEL:2 * PANEL])
    panel_second = lax.linalg.triangular_solve(lower_second, middle[:, PANEL:2 * PANEL], left_side=False, lower=True, transpose_a=True)
    panel_second = panel_second.at[:PANEL].set(0.0).at[PANEL:2 * PANEL].set(lower_second)
    trailing = middle - jnp.dot(panel_second, panel_second.T, precision=EXACT)
    block_ids = positions // PANEL
    trailing = jnp.where((block_ids < 2)[:, None], 0.0, trailing)
    result = trailing.at[:, :PANEL].set(panel_first).at[:, PANEL:2 * PANEL].set(panel_second)
    result = result.reshape(ROW_BLOCKS, N_ROW, PANEL, COL_BLOCKS, N_COL, PANEL)
    return result.transpose(0, 1, 3, 4, 2, 5)
```

```python
import functools

import jax
import jax.numpy as jnp
from jax import lax
from jax.experimental import pallas as pl
from jax.experimental.pallas import tpu as pltpu
from jax.sharding import PartitionSpec as P

RIDGE = 0.5
F32 = jnp.float32
BF16 = jnp.bfloat16


def mm(a, b):
    return jnp.dot(a, b, preferred_element_type=F32)


def mm_nt(a, b):
    return lax.dot_general(a, b, (((1,), (1,)), ((), ())), preferred_element_type=F32)


def mm_tn(a, b):
    return lax.dot_general(a, b, (((0,), (0,)), ((), ())), preferred_element_type=F32)


def split(x):
    high = x.astype(BF16)
    return high, (x - high.astype(F32)).astype(BF16)


def mm3(product, a, b):
    a_high, a_low = a
    b_high, b_low = b
    return product(a_high, b_high) + (product(a_high, b_low) + product(a_low, b_high))


def ordered(raw, order_row):
    size = raw.shape[0]
    source = lax.broadcasted_iota(jnp.int32, (size, size), 0)
    chosen = jnp.where(source == order_row, 1.0, 0.0).astype(BF16)
    return mm_tn(chosen, raw).astype(BF16)


def scale(cand, weights):
    widened = cand.astype(F32)
    scaled = (widened * weights).astype(BF16)
    return scaled, jnp.sum(scaled.astype(F32) * widened, axis=1, keepdims=True)


def as_row(column):
    size = column.shape[0]
    return jnp.transpose(jnp.broadcast_to(column, (size, 128)))[0:8, :]


def tile(scaled, squares, cand, squares_row):
    return jnp.exp(-0.5 * (squares + squares_row - 2.0 * mm_nt(scaled, cand)))


def eye(size):
    rows = lax.broadcasted_iota(jnp.int32, (size, size), 0)
    return rows == lax.broadcasted_iota(jnp.int32, (size, size), 1)


STRIP = 128
MICRO = 8


def factor_strip(work):
    sub = lax.broadcasted_iota(jnp.int32, (MICRO, 128), 0)
    for step in range(STRIP // MICRO):
        base = step * MICRO
        rows = work[base : base + MICRO, :]
        left, right = rows[:, :128], rows[:, 128:]
        lanes = [
            jnp.broadcast_to(left[:, base + j : base + j + 1], (MICRO, 128)) for j in range(MICRO)
        ]
        for k in range(MICRO):
            pivot = lax.rsqrt(jnp.broadcast_to(lanes[k][k : k + 1, :], (MICRO, 128)))
            factor = lanes[k] * pivot
            below = jnp.where(sub > k, factor, 0.0)
            for j in range(k + 1, MICRO):
                lanes[j] = lanes[j] - below * jnp.broadcast_to(factor[j : j + 1, :], (MICRO, 128))
            left_k = left * pivot
            right_k = right * pivot
            left = jnp.where(
                sub == k, left_k, left - below * jnp.broadcast_to(left_k[k : k + 1], (MICRO, 128))
            )
            right = jnp.where(
                sub == k, right_k, right - below * jnp.broadcast_to(right_k[k : k + 1], (MICRO, 128))
            )
        done = jnp.concatenate([left, right], axis=1)
        work[base : base + MICRO, :] = done
        if base + MICRO < STRIP:
            high = done.astype(BF16).astype(F32)
            low = done - high
            rhs = jnp.concatenate([high, low, high], axis=0).astype(BF16)
            left_high, left_low = high[:, :128], low[:, :128]
            lhs = jnp.concatenate(
                [left_high, left_high, left_low, jnp.zeros((128 - 3 * MICRO, 128), F32)], axis=0
            )
            turned = jnp.transpose(lhs)[base + MICRO :, : 3 * MICRO].astype(BF16)
            work[base + MICRO :, :] = work[base + MICRO :, :] - mm(turned, rhs)


def corner_kernel(raw, order, weights, cand_out, squares_out, lower_out, inv_high, inv_low,
                  corner, upper, inverse, work):
    size = raw.shape[1]
    cands, scaleds, squares = [], [], []
    for block in range(2):
        cand = ordered(raw[block], order[block : block + 1, :])
        scaled, square = scale(cand, weights[...])
        cand_out[block * size : (block + 1) * size, :] = cand
        squares_out[:, block * size : (block + 1) * size] = as_row(square)
        cands.append(cand)
        scaleds.append(scaled)
        squares.append(square)
    for block in range(2):
        own = slice(block * size, (block + 1) * size)
        square = tile(scaleds[block], squares[block], cands[block], squares_out[0:1, own])
        square = 0.5 * (square + jnp.transpose(square))
        corner[own, own] = square + jnp.where(eye(size), RIDGE, 0.0)
    cross = tile(scaleds[1], squares[1], cands[0], squares_out[0:1, :size])
    corner[:size, size:] = jnp.transpose(cross)
    corner[size:, :size] = cross
    upper[...] = jnp.zeros_like(upper)
    inverse[...] = jnp.zeros_like(inverse)

    def strip(index, _):
        own = pl.ds(pl.multiple_of(index * STRIP, STRIP), STRIP)
        left = split(jnp.transpose(upper[:, own]))
        current = corner[own, :] - mm3(mm, left, split(upper[...]))
        inverse_part = mm3(mm, left, split(inverse[...]))
        corner[own, :] = current
        work[:, :STRIP] = corner[own, own]
        work[:, STRIP:] = jnp.where(eye(STRIP), 1.0, 0.0)
        factor_strip(work)
        diagonal_inverse = work[:, STRIP:]
        turn = split(diagonal_inverse)
        rows = mm3(mm, turn, split(current))
        column = lax.broadcasted_iota(jnp.int32, rows.shape, 1)
        row = lax.broadcasted_iota(jnp.int32, rows.shape, 0) + index * STRIP
        upper[own, :] = jnp.where(column >= row, rows, 0.0)
        inverse[own, :] = -mm3(mm, turn, split(inverse_part))
        inverse[own, own] = diagonal_inverse
        return 0

    lax.fori_loop(0, corner.shape[0] // STRIP, strip, 0)
    lower_out[...] = jnp.transpose(upper[...])
    high, low = split(inverse[...])
    inv_high[...] = high
    inv_low[...] = low


def corner_call(raw, order, weights):
    size, features = raw.shape[1:]
    whole = 2 * size
    return pl.pallas_call(
        corner_kernel,
        out_shape=(
            jax.ShapeDtypeStruct((whole, features), BF16),
            jax.ShapeDtypeStruct((8, whole), F32),
            jax.ShapeDtypeStruct((whole, whole), F32),
            jax.ShapeDtypeStruct((whole, whole), BF16),
            jax.ShapeDtypeStruct((whole, whole), BF16),
        ),
        scratch_shapes=[
            pltpu.VMEM((whole, whole), F32),
            pltpu.VMEM((whole, whole), F32),
            pltpu.VMEM((whole, whole), F32),
            pltpu.VMEM((STRIP, 2 * STRIP), F32),
        ],
        compiler_params=pltpu.CompilerParams(vmem_limit_bytes=24 << 20),
        cost_estimate=pl.CostEstimate(
            flops=20_000_000_000, bytes_accessed=4 << 20, transcendentals=0
        ),
        name="corner",
    )(raw, order, weights)


def window_kernel(row_count, col_count, place, rows_raw, rows_order, cols_raw, cols_order, weights,
                  lead, lead_squares, lower, inv_high, inv_low, out,
                  col_cand, col_squares, col_high, col_low):
    step = pl.program_id(0)
    row_index, col_index = place[0], place[1]
    size = rows_raw.shape[1]
    local_cols = cols_raw.shape[0]
    label = step * row_count + row_index

    def panel(scaled, squares, block):
        entries = tile(scaled, squares, lead[...], lead_squares[0:1, :])
        inverse = (inv_high[...], inv_low[...])
        solved = mm3(mm_nt, split(entries), inverse)
        start = pl.multiple_of(jnp.minimum(block, 1) * size, size)
        return jnp.where(block < 2, lower[pl.ds(start, size), :], solved)

    @pl.when(step == 0)
    def _():
        for b in range(local_cols):
            own = slice(b * size, (b + 1) * size)
            cand = ordered(cols_raw[b], cols_order[b : b + 1, :])
            scaled, squares = scale(cand, weights[...])
            high, low = split(panel(scaled, squares, b * col_count + col_index))
            col_cand[own, :] = cand
            col_squares[:, own] = as_row(squares)
            col_high[own, :] = high
            col_low[own, :] = low

    cand = ordered(rows_raw[0], rows_order[pl.ds(step, 1), :])
    scaled, squares = scale(cand, weights[...])
    factors = panel(scaled, squares, label)
    halves = split(factors)
    for b in range(local_cols):
        own = slice(b * size, (b + 1) * size)
        column = b * col_count + col_index
        entries = tile(scaled, squares, col_cand[own, :], col_squares[0:1, own])
        entries = entries - mm3(mm_nt, halves, (col_high[own, :], col_low[own, :]))
        ridge = jnp.where(label == column, RIDGE, 0.0)
        entries = entries + jnp.where(eye(size), ridge, 0.0)
        entries = jnp.where(label < 2, 0.0, entries)
        if b == 0:
            lead_part = jnp.where(column == 0, factors[:, :size], factors[:, size:])
            entries = jnp.where(column < 2, lead_part, entries)
        out[0, 0, b, 0] = entries


def window_call(row_count, col_count, place, rows_raw, rows_order, cols_raw, cols_order, weights,
                corner):
    local_rows, size, features = rows_raw.shape
    local_cols = cols_raw.shape[0]
    whole = 2 * size

    def fixed(shape):
        return pl.BlockSpec(shape, lambda i, *_: (0,) * len(shape))

    return pl.pallas_call(
        functools.partial(window_kernel, row_count, col_count),
        out_shape=jax.ShapeDtypeStruct((local_rows, 1, local_cols, 1, size, size), F32),
        grid=(local_rows,),
        in_specs=[
            pl.BlockSpec(memory_space=pltpu.SMEM),
            pl.BlockSpec((1, size, features), lambda i: (i, 0, 0)),
            fixed((local_rows, size)),
            fixed((local_cols, size, features)),
            fixed((local_cols, size)),
            fixed((1, features)),
            fixed((whole, features)),
            fixed((8, whole)),
            fixed((whole, whole)),
            fixed((whole, whole)),
            fixed((whole, whole)),
        ],
        out_specs=pl.BlockSpec(
            (1, 1, local_cols, 1, size, size), lambda i: (i, 0, 0, 0, 0, 0)
        ),
        scratch_shapes=[
            pltpu.VMEM((local_cols * size, features), BF16),
            pltpu.VMEM((8, local_cols * size), F32),
            pltpu.VMEM((local_cols * size, whole), BF16),
            pltpu.VMEM((local_cols * size, whole), BF16),
        ],
        compiler_params=pltpu.CompilerParams(vmem_limit_bytes=40 << 20),
        name="window",
    )(place, rows_raw, rows_order, cols_raw, cols_order, weights, *corner)


def per_device(gradients, feature_weights, order):
    row_count = lax.axis_size("row")
    col_count = lax.axis_size("col")
    row_index = lax.axis_index("row")
    col_index = lax.axis_index("col")
    ratio = col_count // row_count
    local_rows, _, _, part, features = gradients.shape
    size = order.shape[2]
    weights = feature_weights.reshape(1, features)
    orders = lax.all_gather(order, "row", axis=1, tiled=True)
    leaders = lax.all_gather(gradients[0, 0], ("row", "col"), axis=0, tiled=False)
    leaders = leaders.reshape(row_count, size, features)[:2]
    gathered = lax.all_gather(gradients, "col", axis=2, tiled=True)
    rows_raw = gathered.reshape(local_rows, size, features)
    source = col_index % row_count

    def pick(blocks):
        grouped = blocks.reshape((local_rows // ratio, ratio) + blocks.shape[1:])
        return lax.dynamic_index_in_dim(grouped, col_index // row_count, axis=1, keepdims=False)

    kept = jnp.where(row_index == source, pick(rows_raw), 0).astype(BF16)
    cols_raw = lax.psum(kept, "row")
    cols_order = pick(lax.dynamic_index_in_dim(orders, source, axis=1, keepdims=False))
    corner = corner_call(leaders, orders[0, :2], weights)
    place = jnp.stack([row_index, col_index]).astype(jnp.int32)
    return window_call(
        row_count, col_count, place, rows_raw, order.reshape(local_rows, size), cols_raw,
        cols_order, weights, corner,
    )


def solution(mesh):
    placed = (P(None, "row", "col", None, None), P(), P(None, "row", None))
    return jax.shard_map(
        per_device,
        mesh=mesh,
        in_specs=placed,
        out_specs=P(None, "row", None, "col", None, None),
        check_vma=False,
    )
```

```python
import functools

import jax
import jax.numpy as jnp
from jax import lax
from jax.experimental import pallas as pl
from jax.experimental.pallas import tpu as pltpu
from jax.sharding import PartitionSpec as P

RIDGE = 0.5
F32 = jnp.float32
BF16 = jnp.bfloat16


def mm(a, b):
    return jnp.dot(a, b, preferred_element_type=F32)


def mm_nt(a, b):
    return lax.dot_general(a, b, (((1,), (1,)), ((), ())), preferred_element_type=F32)


def mm_tn(a, b):
    return lax.dot_general(a, b, (((0,), (0,)), ((), ())), preferred_element_type=F32)


def split(x):
    high = x.astype(BF16)
    return high, (x - high.astype(F32)).astype(BF16)


def mm3(product, a, b):
    a_high, a_low = a
    b_high, b_low = b
    return product(a_high, b_high) + (product(a_high, b_low) + product(a_low, b_high))


def ordered(raw, order_row):
    size = raw.shape[0]
    source = lax.broadcasted_iota(jnp.int32, (size, size), 0)
    chosen = jnp.where(source == order_row, 1.0, 0.0).astype(BF16)
    return mm_tn(chosen, raw).astype(BF16)


def scale(cand, weights):
    widened = cand.astype(F32)
    scaled = (widened * weights).astype(BF16)
    return scaled, jnp.sum(scaled.astype(F32) * widened, axis=1, keepdims=True)


def as_row(column):
    size = column.shape[0]
    return jnp.transpose(jnp.broadcast_to(column, (size, 128)))[0:8, :]


def tile(scaled, squares, cand, squares_row):
    return jnp.exp(-0.5 * (squares + squares_row - 2.0 * mm_nt(scaled, cand)))


def eye(size):
    rows = lax.broadcasted_iota(jnp.int32, (size, size), 0)
    return rows == lax.broadcasted_iota(jnp.int32, (size, size), 1)


STRIP = 128
MICRO = 8


def factor_strip(work):
    sub = lax.broadcasted_iota(jnp.int32, (MICRO, 128), 0)
    for step in range(STRIP // MICRO):
        base = step * MICRO
        rows = work[base : base + MICRO, :]
        left, right = rows[:, :128], rows[:, 128:]
        lanes = [
            jnp.broadcast_to(left[:, base + j : base + j + 1], (MICRO, 128)) for j in range(MICRO)
        ]
        for k in range(MICRO):
            pivot = lax.rsqrt(jnp.broadcast_to(lanes[k][k : k + 1, :], (MICRO, 128)))
            factor = lanes[k] * pivot
            below = jnp.where(sub > k, factor, 0.0)
            for j in range(k + 1, MICRO):
                lanes[j] = lanes[j] - below * jnp.broadcast_to(factor[j : j + 1, :], (MICRO, 128))
            left_k = left * pivot
            right_k = right * pivot
            left = jnp.where(
                sub == k, left_k, left - below * jnp.broadcast_to(left_k[k : k + 1], (MICRO, 128))
            )
            right = jnp.where(
                sub == k, right_k, right - below * jnp.broadcast_to(right_k[k : k + 1], (MICRO, 128))
            )
        done = jnp.concatenate([left, right], axis=1)
        work[base : base + MICRO, :] = done
        if base + MICRO < STRIP:
            high = done.astype(BF16).astype(F32)
            low = done - high
            rhs = jnp.concatenate([high, low, high], axis=0).astype(BF16)
            left_high, left_low = high[:, :128], low[:, :128]
            lhs = jnp.concatenate(
                [left_high, left_high, left_low, jnp.zeros((128 - 3 * MICRO, 128), F32)], axis=0
            )
            turned = jnp.transpose(lhs)[base + MICRO :, : 3 * MICRO].astype(BF16)
            work[base + MICRO :, :] = work[base + MICRO :, :] - mm(turned, rhs)


def corner_kernel(raw, order, weights, cand_out, squares_out, lower_out, inv_high, inv_low,
                  corner, upper, inverse, work):
    size = raw.shape[1]
    cands, scaleds, squares = [], [], []
    for block in range(2):
        cand = ordered(raw[block], order[block, 0:1, :])
        scaled, square = scale(cand, weights[...])
        cand_out[block * size : (block + 1) * size, :] = cand
        squares_out[:, block * size : (block + 1) * size] = as_row(square)
        cands.append(cand)
        scaleds.append(scaled)
        squares.append(square)
    for block in range(2):
        own = slice(block * size, (block + 1) * size)
        square = tile(scaleds[block], squares[block], cands[block], squares_out[0:1, own])
        square = 0.5 * (square + jnp.transpose(square))
        corner[own, own] = square + jnp.where(eye(size), RIDGE, 0.0)
    cross = tile(scaleds[1], squares[1], cands[0], squares_out[0:1, :size])
    corner[:size, size:] = jnp.transpose(cross)
    corner[size:, :size] = cross
    upper[...] = jnp.zeros_like(upper)
    inverse[...] = jnp.zeros_like(inverse)

    def strip(index, _):
        own = pl.ds(pl.multiple_of(index * STRIP, STRIP), STRIP)
        left = split(jnp.transpose(upper[:, own]))
        current = corner[own, :] - mm3(mm, left, split(upper[...]))
        inverse_part = mm3(mm, left, split(inverse[...]))
        corner[own, :] = current
        work[:, :STRIP] = corner[own, own]
        work[:, STRIP:] = jnp.where(eye(STRIP), 1.0, 0.0)
        factor_strip(work)
        diagonal_inverse = work[:, STRIP:]
        turn = split(diagonal_inverse)
        rows = mm3(mm, turn, split(current))
        column = lax.broadcasted_iota(jnp.int32, rows.shape, 1)
        row = lax.broadcasted_iota(jnp.int32, rows.shape, 0) + index * STRIP
        upper[own, :] = jnp.where(column >= row, rows, 0.0)
        inverse[own, :] = -mm3(mm, turn, split(inverse_part))
        inverse[own, own] = diagonal_inverse
        return 0

    lax.fori_loop(0, corner.shape[0] // STRIP, strip, 0)
    lower_out[...] = jnp.transpose(upper[...])
    high, low = split(inverse[...])
    inv_high[...] = high
    inv_low[...] = low


def corner_call(raw, order, weights):
    size, features = raw.shape[1:]
    whole = 2 * size
    return pl.pallas_call(
        corner_kernel,
        out_shape=(
            jax.ShapeDtypeStruct((whole, features), BF16),
            jax.ShapeDtypeStruct((8, whole), F32),
            jax.ShapeDtypeStruct((whole, whole), F32),
            jax.ShapeDtypeStruct((whole, whole), BF16),
            jax.ShapeDtypeStruct((whole, whole), BF16),
        ),
        scratch_shapes=[
            pltpu.VMEM((whole, whole), F32),
            pltpu.VMEM((whole, whole), F32),
            pltpu.VMEM((whole, whole), F32),
            pltpu.VMEM((STRIP, 2 * STRIP), F32),
        ],
        compiler_params=pltpu.CompilerParams(vmem_limit_bytes=24 << 20),
        cost_estimate=pl.CostEstimate(
            flops=20_000_000_000, bytes_accessed=4 << 20, transcendentals=0
        ),
        name="corner",
    )(raw, order, weights)


def window_kernel(row_count, col_count, rows_raw, orders, cols_raw, weights,
                  lead, lead_squares, lower, inv_high, inv_low, out,
                  col_cand, col_squares, col_high, col_low):
    step = pl.program_id(0)
    row_index, col_index = lax.axis_index("row"), lax.axis_index("col")
    ratio = col_count // row_count
    source, group = lax.rem(col_index, row_count), lax.div(col_index, row_count)
    size = rows_raw.shape[1]
    local_cols = cols_raw.shape[0]
    label = step * row_count + row_index

    def panel(scaled, squares, block):
        entries = tile(scaled, squares, lead[...], lead_squares[0:1, :])
        inverse = (inv_high[...], inv_low[...])
        solved = mm3(mm_nt, split(entries), inverse)
        start = pl.multiple_of(jnp.minimum(block, 1) * size, size)
        return jnp.where(block < 2, lower[pl.ds(start, size), :], solved)

    @pl.when(step == 0)
    def _():
        for b in range(local_cols):
            own = slice(b * size, (b + 1) * size)
            cand = ordered(cols_raw[b], orders[source, pl.ds(b * ratio + group, 1), :])
            scaled, squares = scale(cand, weights[...])
            high, low = split(panel(scaled, squares, b * col_count + col_index))
            col_cand[own, :] = cand
            col_squares[:, own] = as_row(squares)
            col_high[own, :] = high
            col_low[own, :] = low

    cand = ordered(rows_raw[0], orders[row_index, pl.ds(step, 1), :])
    scaled, squares = scale(cand, weights[...])
    factors = panel(scaled, squares, label)
    halves = split(factors)
    for b in range(local_cols):
        own = slice(b * size, (b + 1) * size)
        column = b * col_count + col_index
        entries = tile(scaled, squares, col_cand[own, :], col_squares[0:1, own])
        entries = entries - mm3(mm_nt, halves, (col_high[own, :], col_low[own, :]))
        ridge = jnp.where(label == column, RIDGE, 0.0)
        entries = entries + jnp.where(eye(size), ridge, 0.0)
        entries = jnp.where(label < 2, 0.0, entries)
        if b == 0:
            lead_part = jnp.where(column == 0, factors[:, :size], factors[:, size:])
            entries = jnp.where(column < 2, lead_part, entries)
        out[0, 0, b, 0] = entries


def window_call(row_count, col_count, rows_raw, orders, cols_raw, weights, corner):
    local_rows, size, features = rows_raw.shape
    local_cols = cols_raw.shape[0]
    whole = 2 * size

    def fixed(shape):
        return pl.BlockSpec(shape, lambda i, *_: (0,) * len(shape))

    return pl.pallas_call(
        functools.partial(window_kernel, row_count, col_count),
        out_shape=jax.ShapeDtypeStruct((local_rows, 1, local_cols, 1, size, size), F32),
        grid=(local_rows,),
        in_specs=[
            pl.BlockSpec((1, size, features), lambda i: (i, 0, 0)),
            fixed((row_count, local_rows, size)),
            fixed((local_cols, size, features)),
            fixed((1, features)),
            fixed((whole, features)),
            fixed((8, whole)),
            fixed((whole, whole)),
            fixed((whole, whole)),
            fixed((whole, whole)),
        ],
        out_specs=pl.BlockSpec(
            (1, 1, local_cols, 1, size, size), lambda i: (i, 0, 0, 0, 0, 0)
        ),
        scratch_shapes=[
            pltpu.VMEM((local_cols * size, features), BF16),
            pltpu.VMEM((8, local_cols * size), F32),
            pltpu.VMEM((local_cols * size, whole), BF16),
            pltpu.VMEM((local_cols * size, whole), BF16),
        ],
        compiler_params=pltpu.CompilerParams(vmem_limit_bytes=40 << 20),
        name="window",
    )(rows_raw, orders, cols_raw, weights, *corner)


MESH = pl.DeviceIdType.MESH


def gather_kernel(row_count, col_count, grads, order, rows, cols, leads, orders,
                  lead_send, rows_send, cols_send, order_send,
                  lead_recv, rows_recv, cols_recv, order_recv, local):
    row, col = lax.axis_index("row"), lax.axis_index("col")
    y_count = max(row_count // 2, 1)
    z_count = col_count // y_count
    z, y = lax.div(col, y_count), lax.rem(col, y_count)
    owner = row == lax.rem(col, row_count)
    group = lax.div(col, row_count)
    steps = (
        (z < z_count - 1, col + y_count),
        (z > 0, col - y_count),
        (y < y_count - 1, col + 1),
        (y > 0, col - 1),
    )
    others = [lax.rem(row + k, row_count) for k in range(1, row_count)]

    barrier = pltpu.get_barrier_semaphore()
    expected = row_count - 1
    for other in others:
        pl.semaphore_signal(barrier, inc=1, device_id=(other, col), device_id_type=MESH)
    for inside, neighbour in steps:
        @pl.when(inside)
        def _():
            pl.semaphore_signal(barrier, inc=1, device_id=(row, neighbour), device_id_type=MESH)

        expected = expected + jnp.where(inside, 1, 0)
    pl.semaphore_wait(barrier, expected)

    started = []

    def push(condition, source, target, send, receive, device):
        def copy():
            return pltpu.make_async_remote_copy(
                src_ref=source, dst_ref=target, send_sem=send, recv_sem=receive,
                device_id=device, device_id_type=MESH,
            )

        @pl.when(condition)
        def _():
            copy().start()

        started.append((condition, lambda: copy().wait_send()))

    def keep(condition, source, target, sem):
        def copy():
            return pltpu.make_async_copy(source, target, sem)

        @pl.when(condition)
        def _():
            copy().start()

        started.append((condition, lambda: copy().wait()))

    def arrived(condition, target, receive):
        @pl.when(condition)
        def _():
            pltpu.make_async_remote_copy(
                src_ref=target, dst_ref=target, send_sem=receive, recv_sem=receive,
                device_id=(row, col), device_id_type=MESH,
            ).wait_recv()

    def onward(dz, dy):
        open_ways = []
        if dy == 0 and dz <= 0:
            open_ways.append(0)
        if dy == 0 and dz >= 0:
            open_ways.append(1)
        if dy <= 0:
            open_ways.append(2)
        if dy >= 0:
            open_ways.append(3)
        return open_ways

    offsets = sorted(
        ((dz, dy) for dz in range(1 - z_count, z_count) for dy in range(1 - y_count, y_count)),
        key=lambda o: (abs(o[0]) + abs(o[1]), abs(o[1])),
    )
    true = row >= 0
    leading = row < 2

    def present(dz, dy):
        inside = jnp.logical_and(z + dz >= 0, z + dz < z_count)
        inside = jnp.logical_and(inside, jnp.logical_and(y + dy >= 0, y + dy < y_count))
        slab = (z + dz) * y_count + y + dy
        return inside, jnp.where(inside, slab, 0)

    def lead_event(dz, dy):
        inside, slab = present(dz, dy)
        mine = jnp.logical_and(inside, leading)
        half = jnp.where(leading, row, 0)
        target = leads.at[half, slab]
        first = dz == 0 and dy == 0
        if first:
            keep(mine, grads.at[0, 0], target, local.at[0])
        else:
            arrived(mine, target, lead_recv.at[half, slab])
        source = grads.at[0, 0] if first else target
        for way in onward(dz, dy):
            push(jnp.logical_and(mine, steps[way][0]), source, target,
                 lead_send.at[slab, way], lead_recv.at[half, slab], (row, steps[way][1]))
        for k, other in enumerate(others):
            push(mine, source, target, lead_send.at[slab, 4 + k], lead_recv.at[half, slab],
                 (other, col))

    def rows_event(dz, dy):
        inside, slab = present(dz, dy)
        target = rows.at[:, :, slab]
        first = dz == 0 and dy == 0
        if first:
            keep(true, grads, target, local.at[1])
        else:
            arrived(inside, target, rows_recv.at[slab])
        source = grads if first else target
        for way in onward(dz, dy):
            push(jnp.logical_and(inside, steps[way][0]), source, target,
                 rows_send.at[slab, way], rows_recv.at[slab], (row, steps[way][1]))
        forward = jnp.logical_and(inside, owner)
        picked = grads.at[:, group] if first else rows.at[:, group, slab]
        for k, other in enumerate(others):
            push(forward, picked, cols.at[:, slab], cols_send.at[slab, k], cols_recv.at[slab],
                 (other, col))
        keep(forward, picked, cols.at[:, slab], cols_send.at[slab, row_count - 1])

    lead_event(0, 0)
    for k, other in enumerate(others):
        push(true, order, orders.at[row], order_send.at[k], order_recv.at[row], (other, col))
    keep(true, order, orders.at[row], local.at[2])
    rows_event(0, 0)
    for offset in offsets[1:]:
        lead_event(*offset)
    for offset in offsets[1:]:
        rows_event(*offset)
    for half in range(2):
        for slab in range(col_count):
            arrived(row != half, leads.at[half, slab], lead_recv.at[half, slab])
    for other in others:
        arrived(true, orders.at[other], order_recv.at[other])
    for slab in range(col_count):
        arrived(jnp.logical_not(owner), cols.at[:, slab], cols_recv.at[slab])
    for condition, finish in started:
        pl.when(condition)(finish)


def gather_call(row_count, col_count, grads, order):
    local_cols, ratio, part, features = grads.shape
    local_rows, size = order.shape
    hbm = pl.BlockSpec(memory_space=pl.ANY)
    dma = pltpu.SemaphoreType.DMA
    return pl.pallas_call(
        functools.partial(gather_kernel, row_count, col_count),
        out_shape=(
            jax.ShapeDtypeStruct((local_cols, ratio, col_count, part, features), BF16),
            jax.ShapeDtypeStruct((local_cols, col_count, part, features), BF16),
            jax.ShapeDtypeStruct((2, col_count, part, features), BF16),
            jax.ShapeDtypeStruct((row_count, local_rows, size), jnp.int32),
        ),
        in_specs=[hbm, hbm],
        out_specs=(hbm, hbm, hbm, hbm),
        scratch_shapes=[
            dma((col_count, 3 + row_count)),
            dma((col_count, 4)),
            dma((col_count, row_count)),
            dma((row_count,)),
            dma((2, col_count)),
            dma((col_count,)),
            dma((col_count,)),
            dma((row_count,)),
            dma((3,)),
        ],
        compiler_params=pltpu.CompilerParams(collective_id=0, has_side_effects=True),
        name="gather",
    )(grads, order)


def per_device(gradients, feature_weights, order):
    row_count = lax.axis_size("row")
    col_count = lax.axis_size("col")
    ratio = col_count // row_count
    local_rows, _, _, part, features = gradients.shape
    size = order.shape[2]
    weights = feature_weights.reshape(1, features)
    rows, cols, leads, orders = gather_call(
        row_count, col_count, gradients.reshape(local_rows // ratio, ratio, part, features),
        order.reshape(local_rows, size),
    )
    corner = corner_call(leads.reshape(2, size, features), orders, weights)
    return window_call(
        row_count, col_count, rows.reshape(local_rows, size, features), orders,
        cols.reshape(local_rows // ratio, size, features), weights, corner,
    )


def solution(mesh):
    placed = (P(None, "row", "col", None, None), P(), P(None, "row", None))
    return jax.shard_map(
        per_device,
        mesh=mesh,
        in_specs=placed,
        out_specs=P(None, "row", None, "col", None, None),
        check_vma=False,
    )
```

```python
import functools

import jax
import jax.numpy as jnp
from jax import lax
from jax.experimental import pallas as pl
from jax.experimental.pallas import tpu as pltpu
from jax.sharding import PartitionSpec as P

RIDGE = 0.5
F32 = jnp.float32
BF16 = jnp.bfloat16


def mm(a, b):
    return jnp.dot(a, b, preferred_element_type=F32)


def mm_nt(a, b):
    return lax.dot_general(a, b, (((1,), (1,)), ((), ())), preferred_element_type=F32)


def mm_tn(a, b):
    return lax.dot_general(a, b, (((0,), (0,)), ((), ())), preferred_element_type=F32)


def split(x):
    high = x.astype(BF16)
    return high, (x - high.astype(F32)).astype(BF16)


def mm3(product, a, b):
    a_high, a_low = a
    b_high, b_low = b
    return product(a_high, b_high) + (product(a_high, b_low) + product(a_low, b_high))


def ordered(raw, order_row):
    size = raw.shape[0]
    source = lax.broadcasted_iota(jnp.int32, (size, size), 0)
    chosen = jnp.where(source == order_row, 1.0, 0.0).astype(BF16)
    return mm_tn(chosen, raw).astype(BF16)


def scale(cand, weights):
    widened = cand.astype(F32)
    scaled = (widened * weights).astype(BF16)
    return scaled, jnp.sum(scaled.astype(F32) * widened, axis=1, keepdims=True)


def as_row(column):
    size = column.shape[0]
    return jnp.transpose(jnp.broadcast_to(column, (size, 128)))[0:8, :]


def tile(scaled, squares, cand, squares_row):
    return jnp.exp(-0.5 * (squares + squares_row - 2.0 * mm_nt(scaled, cand)))


def eye(size):
    rows = lax.broadcasted_iota(jnp.int32, (size, size), 0)
    return rows == lax.broadcasted_iota(jnp.int32, (size, size), 1)


STRIP = 128
MICRO = 16


def factor_strip(work):
    sub = lax.broadcasted_iota(jnp.int32, (MICRO, 128), 0)
    for step in range(STRIP // MICRO):
        base = step * MICRO
        rows = work[base : base + MICRO, :]
        left, right = rows[:, :128], rows[:, 128:]
        lanes = [
            jnp.broadcast_to(left[:, base + j : base + j + 1], (MICRO, 128)) for j in range(MICRO)
        ]
        for k in range(MICRO):
            pivot = lax.rsqrt(jnp.broadcast_to(lanes[k][k : k + 1, :], (MICRO, 128)))
            below = jnp.where(sub > k, lanes[k], 0.0) * (pivot * pivot)
            for j in range(k + 1, MICRO):
                lanes[j] = lanes[j] - below * jnp.broadcast_to(lanes[k][j : j + 1, :], (MICRO, 128))
            left = jnp.where(
                sub == k,
                left * pivot,
                left - below * jnp.broadcast_to(left[k : k + 1], (MICRO, 128)),
            )
            right = jnp.where(
                sub == k,
                right * pivot,
                right - below * jnp.broadcast_to(right[k : k + 1], (MICRO, 128)),
            )
        done = jnp.concatenate([left, right], axis=1)
        work[base : base + MICRO, :] = done
        if base + MICRO < STRIP:
            high = done.astype(BF16).astype(F32)
            low = done - high
            rhs = jnp.concatenate([high, low, high], axis=0).astype(BF16)
            left_high, left_low = high[:, :128], low[:, :128]
            lhs = jnp.concatenate(
                [left_high, left_high, left_low, jnp.zeros((128 - 3 * MICRO, 128), F32)], axis=0
            )
            turned = jnp.transpose(lhs)[base + MICRO :, : 3 * MICRO].astype(BF16)
            work[base + MICRO :, :] = work[base + MICRO :, :] - mm(turned, rhs)


def corner_body(raw, order, weights, cand_out, squares_out, lower_out, inv_high, inv_low,
                corner, upper, inverse, work, meanwhile):
    size = raw.shape[1] * raw.shape[2]
    cands, scaleds, squares = [], [], []
    for block in range(2):
        cand = ordered(raw[block].reshape(size, raw.shape[3]), order[block, 0:1, :])
        scaled, square = scale(cand, weights[...])
        cand_out[block * size : (block + 1) * size, :] = cand
        squares_out[:, block * size : (block + 1) * size] = as_row(square)
        cands.append(cand)
        scaleds.append(scaled)
        squares.append(square)
    for block in range(2):
        own = slice(block * size, (block + 1) * size)
        square = tile(scaleds[block], squares[block], cands[block], squares_out[0:1, own])
        square = 0.5 * (square + jnp.transpose(square))
        corner[own, own] = square + jnp.where(eye(size), RIDGE, 0.0)
    cross = tile(scaleds[1], squares[1], cands[0], squares_out[0:1, :size])
    corner[:size, size:] = jnp.transpose(cross)
    corner[size:, :size] = cross
    upper[...] = jnp.zeros_like(upper)
    inverse[...] = jnp.zeros_like(inverse)

    def strip(index, _):
        meanwhile(index)
        own = pl.ds(pl.multiple_of(index * STRIP, STRIP), STRIP)
        left = split(jnp.transpose(upper[:, own]))
        current = corner[own, :] - mm3(mm, left, split(upper[...]))
        inverse_part = mm3(mm, left, split(inverse[...]))
        corner[own, :] = current
        work[:, :STRIP] = corner[own, own]
        work[:, STRIP:] = jnp.where(eye(STRIP), 1.0, 0.0)
        factor_strip(work)
        diagonal_inverse = work[:, STRIP:]
        turn = split(diagonal_inverse)
        rows = mm3(mm, turn, split(current))
        column = lax.broadcasted_iota(jnp.int32, rows.shape, 1)
        row = lax.broadcasted_iota(jnp.int32, rows.shape, 0) + index * STRIP
        upper[own, :] = jnp.where(column >= row, rows, 0.0)
        inverse[own, :] = -mm3(mm, turn, split(inverse_part))
        inverse[own, own] = diagonal_inverse
        return 0

    lax.fori_loop(0, corner.shape[0] // STRIP, strip, 0)
    lower_out[...] = jnp.transpose(upper[...])
    high, low = split(inverse[...])
    inv_high[...] = high
    inv_low[...] = low


def window_kernel(row_count, col_count, rows_raw, orders, cols_raw, weights,
                  lead, lead_squares, lower, inv_high, inv_low, out,
                  col_cand, col_squares, col_high, col_low):
    step = pl.program_id(0)
    row_index, col_index = lax.axis_index("row"), lax.axis_index("col")
    ratio = col_count // row_count
    source, group = lax.rem(col_index, row_count), lax.div(col_index, row_count)
    size = rows_raw.shape[1]
    local_cols = cols_raw.shape[0]
    label = step * row_count + row_index

    def panel(scaled, squares, block):
        entries = tile(scaled, squares, lead[...], lead_squares[0:1, :])
        high, low = split(entries)
        top, bottom = slice(0, size), slice(size, 2 * size)
        solved = jnp.concatenate(
            [
                mm3(mm_nt, (high[:, top], low[:, top]), (inv_high[top, top], inv_low[top, top])),
                mm3(mm_nt, (high, low), (inv_high[bottom, :], inv_low[bottom, :])),
            ],
            axis=1,
        )
        start = pl.multiple_of(jnp.minimum(block, 1) * size, size)
        return jnp.where(block < 2, lower[pl.ds(start, size), :], solved)

    @pl.when(step == 0)
    def _():
        for b in range(local_cols):
            own = slice(b * size, (b + 1) * size)
            cand = ordered(cols_raw[b], orders[source, pl.ds(b * ratio + group, 1), :])
            scaled, squares = scale(cand, weights[...])
            high, low = split(panel(scaled, squares, b * col_count + col_index))
            col_cand[own, :] = cand
            col_squares[:, own] = as_row(squares)
            col_high[own, :] = high
            col_low[own, :] = low

    cand = ordered(rows_raw[0], orders[row_index, pl.ds(step, 1), :])
    scaled, squares = scale(cand, weights[...])
    factors = panel(scaled, squares, label)
    halves = split(factors)
    for b in range(local_cols):
        own = slice(b * size, (b + 1) * size)
        column = b * col_count + col_index
        entries = tile(scaled, squares, col_cand[own, :], col_squares[0:1, own])
        entries = entries - mm3(mm_nt, halves, (col_high[own, :], col_low[own, :]))
        ridge = jnp.where(label == column, RIDGE, 0.0)
        entries = entries + jnp.where(eye(size), ridge, 0.0)
        entries = jnp.where(label < 2, 0.0, entries)
        if b == 0:
            lead_part = jnp.where(column == 0, factors[:, :size], factors[:, size:])
            entries = jnp.where(column < 2, lead_part, entries)
        out[0, 0, b, 0] = entries


def window_call(row_count, col_count, rows_raw, orders, cols_raw, weights, corner):
    local_rows, size, features = rows_raw.shape
    local_cols = cols_raw.shape[0]
    whole = 2 * size

    def fixed(shape):
        return pl.BlockSpec(shape, lambda i, *_: (0,) * len(shape))

    return pl.pallas_call(
        functools.partial(window_kernel, row_count, col_count),
        out_shape=jax.ShapeDtypeStruct((local_rows, 1, local_cols, 1, size, size), F32),
        grid=(local_rows,),
        in_specs=[
            pl.BlockSpec((1, size, features), lambda i: (i, 0, 0)),
            fixed((row_count, local_rows, size)),
            fixed((local_cols, size, features)),
            fixed((1, features)),
            fixed((whole, features)),
            fixed((8, whole)),
            fixed((whole, whole)),
            fixed((whole, whole)),
            fixed((whole, whole)),
        ],
        out_specs=pl.BlockSpec(
            (1, 1, local_cols, 1, size, size), lambda i: (i, 0, 0, 0, 0, 0)
        ),
        scratch_shapes=[
            pltpu.VMEM((local_cols * size, features), BF16),
            pltpu.VMEM((8, local_cols * size), F32),
            pltpu.VMEM((local_cols * size, whole), BF16),
            pltpu.VMEM((local_cols * size, whole), BF16),
        ],
        compiler_params=pltpu.CompilerParams(vmem_limit_bytes=40 << 20),
        name="window",
    )(rows_raw, orders, cols_raw, weights, *corner)


MESH = pl.DeviceIdType.MESH


def gather_kernel(row_count, col_count, grads, order, weights, rows, cols, orders,
                  cand_out, squares_out, lower_out, inv_high, inv_low,
                  leads, corner, upper, inverse, work,
                  lead_send, rows_send, cols_send, order_send,
                  lead_recv, rows_recv, cols_recv, order_recv, local):
    row, col = lax.axis_index("row"), lax.axis_index("col")
    y_count = max(row_count // 2, 1)
    z_count = col_count // y_count
    z, y = lax.div(col, y_count), lax.rem(col, y_count)
    owner = row == lax.rem(col, row_count)
    group = lax.div(col, row_count)
    steps = (
        (z < z_count - 1, col + y_count),
        (z > 0, col - y_count),
        (y < y_count - 1, col + 1),
        (y > 0, col - 1),
    )
    others = [lax.rem(row + k, row_count) for k in range(1, row_count)]

    barrier = pltpu.get_barrier_semaphore()
    expected = row_count - 1
    for other in others:
        pl.semaphore_signal(barrier, inc=1, device_id=(other, col), device_id_type=MESH)
    for inside, neighbour in steps:
        @pl.when(inside)
        def _():
            pl.semaphore_signal(barrier, inc=1, device_id=(row, neighbour), device_id_type=MESH)

        expected = expected + jnp.where(inside, 1, 0)
    pl.semaphore_wait(barrier, expected)

    def push(finish, condition, source, target, send, receive, device):
        @pl.when(condition)
        def _():
            copy = pltpu.make_async_remote_copy(
                src_ref=source, dst_ref=target, send_sem=send, recv_sem=receive,
                device_id=device, device_id_type=MESH,
            )
            copy.wait_send() if finish else copy.start()

    def keep(finish, condition, source, target, sem):
        @pl.when(condition)
        def _():
            copy = pltpu.make_async_copy(source, target, sem)
            copy.wait() if finish else copy.start()

    def arrived(condition, target, receive):
        @pl.when(condition)
        def _():
            pltpu.make_async_remote_copy(
                src_ref=target, dst_ref=target, send_sem=receive, recv_sem=receive,
                device_id=(row, col), device_id_type=MESH,
            ).wait_recv()

    def onward(dz, dy):
        open_ways = []
        if dy == 0 and dz <= 0:
            open_ways.append(0)
        if dy == 0 and dz >= 0:
            open_ways.append(1)
        if dy <= 0:
            open_ways.append(2)
        if dy >= 0:
            open_ways.append(3)
        return open_ways

    offsets = sorted(
        ((dz, dy) for dz in range(1 - z_count, z_count) for dy in range(1 - y_count, y_count)),
        key=lambda o: (abs(o[0]) + abs(o[1]), abs(o[1])),
    )
    true = row >= 0
    leading = row < 2

    def present(dz, dy):
        inside = jnp.logical_and(z + dz >= 0, z + dz < z_count)
        inside = jnp.logical_and(inside, jnp.logical_and(y + dy >= 0, y + dy < y_count))
        slab = (z + dz) * y_count + y + dy
        return inside, jnp.where(inside, slab, 0)

    def lead_event(dz, dy, finish=False):
        inside, slab = present(dz, dy)
        mine = jnp.logical_and(inside, leading)
        half = jnp.where(leading, row, 0)
        target = leads.at[half, slab]
        first = dz == 0 and dy == 0
        if first:
            keep(finish, mine, grads.at[0, 0], target, local.at[0])
        elif not finish:
            arrived(mine, target, lead_recv.at[half, slab])
        source = grads.at[0, 0] if first else target
        for way in onward(dz, dy):
            push(finish, jnp.logical_and(mine, steps[way][0]), source, target,
                 lead_send.at[slab, way], lead_recv.at[half, slab], (row, steps[way][1]))
        for k, other in enumerate(others):
            push(finish, mine, source, target, lead_send.at[slab, 4 + k], lead_recv.at[half, slab],
                 (other, col))

    def rows_event(dz, dy, finish=False):
        inside, slab = present(dz, dy)
        target = rows.at[:, :, slab]
        first = dz == 0 and dy == 0
        if first:
            keep(finish, true, grads, target, local.at[1])
        elif not finish:
            arrived(inside, target, rows_recv.at[slab])
        source = grads if first else target
        for way in onward(dz, dy):
            push(finish, jnp.logical_and(inside, steps[way][0]), source, target,
                 rows_send.at[slab, way], rows_recv.at[slab], (row, steps[way][1]))
        forward = jnp.logical_and(inside, owner)
        picked = grads.at[:, group] if first else rows.at[:, group, slab]
        for k, other in enumerate(others):
            push(finish, forward, picked, cols.at[:, slab], cols_send.at[slab, k], cols_recv.at[slab],
                 (other, col))
        keep(finish, forward, picked, cols.at[:, slab], cols_send.at[slab, row_count - 1])

    def order_event(finish=False):
        for k, other in enumerate(others):
            push(finish, true, order, orders.at[row], order_send.at[k], order_recv.at[row],
                 (other, col))
        keep(finish, true, order, orders.at[row], local.at[2])

    lead_event(0, 0)
    order_event()
    rows_event(0, 0)
    for offset in offsets[1:]:
        lead_event(*offset)
    for half in range(2):
        for slab in range(col_count):
            arrived(row != half, leads.at[half, slab], lead_recv.at[half, slab])
    for other in others:
        arrived(true, orders.at[other], order_recv.at[other])
    for offset in offsets:
        lead_event(*offset, finish=True)
    order_event(finish=True)
    strips = corner.shape[0] // STRIP

    def meanwhile(index):
        for turn in range(strips):
            @pl.when(index == turn)
            def _():
                for offset in offsets[1:]:
                    if min(abs(offset[0]) + abs(offset[1]), strips) == turn + 1:
                        rows_event(*offset)

    corner_body(leads, orders, weights, cand_out, squares_out, lower_out, inv_high, inv_low,
                corner, upper, inverse, work, meanwhile)
    for slab in range(col_count):
        arrived(jnp.logical_not(owner), cols.at[:, slab], cols_recv.at[slab])
    for offset in offsets:
        rows_event(*offset, finish=True)


def gather_call(row_count, col_count, grads, order, weights):
    local_cols, ratio, part, features = grads.shape
    local_rows, size = order.shape
    whole = 2 * size
    hbm = pl.BlockSpec(memory_space=pl.ANY)
    vmem = pl.BlockSpec(memory_space=pltpu.VMEM)
    dma = pltpu.SemaphoreType.DMA
    return pl.pallas_call(
        functools.partial(gather_kernel, row_count, col_count),
        out_shape=(
            jax.ShapeDtypeStruct((local_cols, ratio, col_count, part, features), BF16),
            jax.ShapeDtypeStruct((local_cols, col_count, part, features), BF16),
            jax.ShapeDtypeStruct((row_count, local_rows, size), jnp.int32),
            jax.ShapeDtypeStruct((whole, features), BF16),
            jax.ShapeDtypeStruct((8, whole), F32),
            jax.ShapeDtypeStruct((whole, whole), F32),
            jax.ShapeDtypeStruct((whole, whole), BF16),
            jax.ShapeDtypeStruct((whole, whole), BF16),
        ),
        in_specs=[hbm, hbm, vmem],
        out_specs=(hbm, hbm, vmem, vmem, vmem, vmem, vmem, vmem),
        scratch_shapes=[
            pltpu.VMEM((2, col_count, part, features), BF16),
            pltpu.VMEM((whole, whole), F32),
            pltpu.VMEM((whole, whole), F32),
            pltpu.VMEM((whole, whole), F32),
            pltpu.VMEM((STRIP, 2 * STRIP), F32),
            dma((col_count, 3 + row_count)),
            dma((col_count, 4)),
            dma((col_count, row_count)),
            dma((row_count,)),
            dma((2, col_count)),
            dma((col_count,)),
            dma((col_count,)),
            dma((row_count,)),
            dma((3,)),
        ],
        compiler_params=pltpu.CompilerParams(
            collective_id=0, has_side_effects=True, vmem_limit_bytes=32 << 20
        ),
        name="gather",
    )(grads, order, weights)


def per_device(gradients, feature_weights, order):
    row_count = lax.axis_size("row")
    col_count = lax.axis_size("col")
    ratio = col_count // row_count
    local_rows, _, _, part, features = gradients.shape
    size = order.shape[2]
    weights = feature_weights.reshape(1, features)
    rows, cols, orders, *corner = gather_call(
        row_count, col_count, gradients.reshape(local_rows // ratio, ratio, part, features),
        order.reshape(local_rows, size), weights,
    )
    return window_call(
        row_count, col_count, rows.reshape(local_rows, size, features), orders,
        cols.reshape(local_rows // ratio, size, features), weights, corner,
    )


def solution(mesh):
    placed = (P(None, "row", "col", None, None), P(), P(None, "row", None))
    return jax.shard_map(
        per_device,
        mesh=mesh,
        in_specs=placed,
        out_specs=P(None, "row", None, "col", None, None),
        check_vma=False,
    )
```

```python
import functools

import jax
import jax.numpy as jnp
from jax import lax
from jax.experimental import pallas as pl
from jax.experimental.pallas import tpu as pltpu
from jax.sharding import PartitionSpec as P

RIDGE = 0.5
F32 = jnp.float32
BF16 = jnp.bfloat16


def mm(a, b):
    return jnp.dot(a, b, preferred_element_type=F32)


def mm_nt(a, b):
    return lax.dot_general(a, b, (((1,), (1,)), ((), ())), preferred_element_type=F32)


def mm_tn(a, b):
    return lax.dot_general(a, b, (((0,), (0,)), ((), ())), preferred_element_type=F32)


def split(x):
    high = x.astype(BF16)
    return high, (x - high.astype(F32)).astype(BF16)


def mm3(product, a, b):
    a_high, a_low = a
    b_high, b_low = b
    return product(a_high, b_high) + (product(a_high, b_low) + product(a_low, b_high))


def ordered(raw, order_row):
    size = raw.shape[0]
    source = lax.broadcasted_iota(jnp.int32, (size, size), 0)
    chosen = jnp.where(source == order_row, 1.0, 0.0).astype(BF16)
    return mm_tn(chosen, raw).astype(BF16)


def scale(cand, weights):
    widened = cand.astype(F32)
    scaled = (widened * weights).astype(BF16)
    return scaled, jnp.sum(scaled.astype(F32) * widened, axis=1, keepdims=True)


def as_row(column):
    size = column.shape[0]
    return jnp.transpose(jnp.broadcast_to(column, (size, 128)))[0:8, :]


def tile(scaled, squares, cand, squares_row):
    return jnp.exp(-0.5 * (squares + squares_row - 2.0 * mm_nt(scaled, cand)))


def eye(size):
    rows = lax.broadcasted_iota(jnp.int32, (size, size), 0)
    return rows == lax.broadcasted_iota(jnp.int32, (size, size), 1)


STRIP = 128
MICRO = 16


def factor_strip(work):
    sub = lax.broadcasted_iota(jnp.int32, (MICRO, 128), 0)
    for step in range(STRIP // MICRO):
        base = step * MICRO
        rows = work[base : base + MICRO, :]
        left, right = rows[:, :128], rows[:, 128:]
        lanes = [
            jnp.broadcast_to(left[:, base + j : base + j + 1], (MICRO, 128)) for j in range(MICRO)
        ]
        for k in range(MICRO):
            pivot = lax.rsqrt(jnp.broadcast_to(lanes[k][k : k + 1, :], (MICRO, 128)))
            below = jnp.where(sub > k, lanes[k], 0.0) * (pivot * pivot)
            for j in range(k + 1, MICRO):
                lanes[j] = lanes[j] - below * jnp.broadcast_to(lanes[k][j : j + 1, :], (MICRO, 128))
            left = jnp.where(
                sub == k,
                left * pivot,
                left - below * jnp.broadcast_to(left[k : k + 1], (MICRO, 128)),
            )
            right = jnp.where(
                sub == k,
                right * pivot,
                right - below * jnp.broadcast_to(right[k : k + 1], (MICRO, 128)),
            )
        done = jnp.concatenate([left, right], axis=1)
        work[base : base + MICRO, :] = done
        if base + MICRO < STRIP:
            high = done.astype(BF16).astype(F32)
            low = done - high
            rhs = jnp.concatenate([high, low, high], axis=0).astype(BF16)
            left_high, left_low = high[:, :128], low[:, :128]
            lhs = jnp.concatenate(
                [left_high, left_high, left_low, jnp.zeros((128 - 3 * MICRO, 128), F32)], axis=0
            )
            turned = jnp.transpose(lhs)[base + MICRO :, : 3 * MICRO].astype(BF16)
            work[base + MICRO :, :] = work[base + MICRO :, :] - mm(turned, rhs)


def corner_body(raw, order, weights, cand_out, squares_out, lower_out, inv_high, inv_low,
                corner, upper, inverse, work, meanwhile):
    size = raw.shape[1] * raw.shape[2]
    cands, scaleds, squares = [], [], []
    for block in range(2):
        cand = ordered(raw[block].reshape(size, raw.shape[3]), order[block, 0:1, :])
        scaled, square = scale(cand, weights[...])
        cand_out[block * size : (block + 1) * size, :] = cand
        squares_out[:, block * size : (block + 1) * size] = as_row(square)
        cands.append(cand)
        scaleds.append(scaled)
        squares.append(square)
    for block in range(2):
        own = slice(block * size, (block + 1) * size)
        square = tile(scaleds[block], squares[block], cands[block], squares_out[0:1, own])
        square = 0.5 * (square + jnp.transpose(square))
        corner[own, own] = square + jnp.where(eye(size), RIDGE, 0.0)
    cross = tile(scaleds[1], squares[1], cands[0], squares_out[0:1, :size])
    corner[:size, size:] = jnp.transpose(cross)
    corner[size:, :size] = cross
    upper[...] = jnp.zeros_like(upper)
    inverse[...] = jnp.zeros_like(inverse)

    def strip(index, _):
        meanwhile(index)
        own = pl.ds(pl.multiple_of(index * STRIP, STRIP), STRIP)
        left = split(jnp.transpose(upper[:, own]))
        current = corner[own, :] - mm3(mm, left, split(upper[...]))
        inverse_part = mm3(mm, left, split(inverse[...]))
        corner[own, :] = current
        work[:, :STRIP] = corner[own, own]
        work[:, STRIP:] = jnp.where(eye(STRIP), 1.0, 0.0)
        factor_strip(work)
        diagonal_inverse = work[:, STRIP:]
        turn = split(diagonal_inverse)
        rows = mm3(mm, turn, split(current))
        column = lax.broadcasted_iota(jnp.int32, rows.shape, 1)
        row = lax.broadcasted_iota(jnp.int32, rows.shape, 0) + index * STRIP
        upper[own, :] = jnp.where(column >= row, rows, 0.0)
        inverse[own, :] = -mm3(mm, turn, split(inverse_part))
        inverse[own, own] = diagonal_inverse
        return 0

    lax.fori_loop(0, corner.shape[0] // STRIP, strip, 0)
    lower_out[...] = jnp.transpose(upper[...])
    high, low = split(inverse[...])
    inv_high[...] = high
    inv_low[...] = low


def window_kernel(row_count, col_count, rows_raw, orders, cols_raw, weights,
                  lead, lead_squares, lower, inv_high, inv_low, out,
                  col_cand, col_squares, col_stack, inv_first, inv_second):
    step = pl.program_id(0)
    row_index, col_index = lax.axis_index("row"), lax.axis_index("col")
    ratio = col_count // row_count
    source, group = lax.rem(col_index, row_count), lax.div(col_index, row_count)
    size = rows_raw.shape[1]
    local_cols = cols_raw.shape[0]
    label = step * row_count + row_index

    def panel(scaled, squares, block):
        entries = tile(scaled, squares, lead[...], lead_squares[0:1, :])
        high, low = split(entries)
        stacked = jnp.concatenate([high[:, :size], high[:, :size], low[:, :size]], axis=1)
        first = mm_nt(stacked, inv_first[...])
        second = mm_nt(jnp.concatenate([high, high, low], axis=1), inv_second[...])
        solved = jnp.concatenate([first, second], axis=1)
        start = pl.multiple_of(jnp.minimum(block, 1) * size, size)
        return jnp.where(block < 2, lower[pl.ds(start, size), :], solved)

    @pl.when(step == 0)
    def _():
        top, bottom = slice(0, size), slice(size, 2 * size)
        inv_first[...] = jnp.concatenate(
            [inv_high[top, top], inv_low[top, top], inv_high[top, top]], axis=1
        )
        inv_second[...] = jnp.concatenate(
            [inv_high[bottom, :], inv_low[bottom, :], inv_high[bottom, :]], axis=1
        )
        for b in range(local_cols):
            own = slice(b * size, (b + 1) * size)
            cand = ordered(cols_raw[b], orders[source, pl.ds(b * ratio + group, 1), :])
            scaled, squares = scale(cand, weights[...])
            high, low = split(panel(scaled, squares, b * col_count + col_index))
            col_cand[own, :] = cand
            col_squares[:, own] = as_row(squares)
            col_stack[own, :] = jnp.concatenate([high, low, high], axis=1)

    cand = ordered(rows_raw[0], orders[row_index, pl.ds(step, 1), :])
    scaled, squares = scale(cand, weights[...])
    factors = panel(scaled, squares, label)
    high, low = split(factors)
    halves = jnp.concatenate([high, high, low], axis=1)
    for b in range(local_cols):
        own = slice(b * size, (b + 1) * size)
        column = b * col_count + col_index
        entries = tile(scaled, squares, col_cand[own, :], col_squares[0:1, own])
        entries = entries - mm_nt(halves, col_stack[own, :])
        ridge = jnp.where(label == column, RIDGE, 0.0)
        entries = entries + jnp.where(eye(size), ridge, 0.0)
        entries = jnp.where(label < 2, 0.0, entries)
        if b == 0:
            lead_part = jnp.where(column == 0, factors[:, :size], factors[:, size:])
            entries = jnp.where(column < 2, lead_part, entries)
        out[0, 0, b, 0] = entries


def window_call(row_count, col_count, rows_raw, orders, cols_raw, weights, corner):
    local_rows, size, features = rows_raw.shape
    local_cols = cols_raw.shape[0]
    whole = 2 * size

    def fixed(shape):
        return pl.BlockSpec(shape, lambda i, *_: (0,) * len(shape))

    return pl.pallas_call(
        functools.partial(window_kernel, row_count, col_count),
        out_shape=jax.ShapeDtypeStruct((local_rows, 1, local_cols, 1, size, size), F32),
        grid=(local_rows,),
        in_specs=[
            pl.BlockSpec((1, size, features), lambda i: (i, 0, 0)),
            fixed((row_count, local_rows, size)),
            fixed((local_cols, size, features)),
            fixed((1, features)),
            fixed((whole, features)),
            fixed((8, whole)),
            fixed((whole, whole)),
            fixed((whole, whole)),
            fixed((whole, whole)),
        ],
        out_specs=pl.BlockSpec(
            (1, 1, local_cols, 1, size, size), lambda i: (i, 0, 0, 0, 0, 0)
        ),
        scratch_shapes=[
            pltpu.VMEM((local_cols * size, features), BF16),
            pltpu.VMEM((8, local_cols * size), F32),
            pltpu.VMEM((local_cols * size, 3 * whole), BF16),
            pltpu.VMEM((size, 3 * size), BF16),
            pltpu.VMEM((size, 3 * whole), BF16),
        ],
        compiler_params=pltpu.CompilerParams(vmem_limit_bytes=40 << 20),
        name="window",
    )(rows_raw, orders, cols_raw, weights, *corner)


MESH = pl.DeviceIdType.MESH


def gather_kernel(row_count, col_count, grads, order, weights, rows, cols, orders,
                  cand_out, squares_out, lower_out, inv_high, inv_low,
                  leads, corner, upper, inverse, work,
                  lead_send, rows_send, cols_send, order_send,
                  lead_recv, rows_recv, cols_recv, order_recv, local):
    row, col = lax.axis_index("row"), lax.axis_index("col")
    y_count = max(row_count // 2, 1)
    z_count = col_count // y_count
    z, y = lax.div(col, y_count), lax.rem(col, y_count)
    owner = row == lax.rem(col, row_count)
    group = lax.div(col, row_count)
    steps = (
        (z < z_count - 1, col + y_count),
        (z > 0, col - y_count),
        (y < y_count - 1, col + 1),
        (y > 0, col - 1),
    )
    others = [lax.rem(row + k, row_count) for k in range(1, row_count)]

    barrier = pltpu.get_barrier_semaphore()
    expected = row_count - 1
    for other in others:
        pl.semaphore_signal(barrier, inc=1, device_id=(other, col), device_id_type=MESH)
    for inside, neighbour in steps:
        @pl.when(inside)
        def _():
            pl.semaphore_signal(barrier, inc=1, device_id=(row, neighbour), device_id_type=MESH)

        expected = expected + jnp.where(inside, 1, 0)
    pl.semaphore_wait(barrier, expected)

    def push(finish, condition, source, target, send, receive, device):
        @pl.when(condition)
        def _():
            copy = pltpu.make_async_remote_copy(
                src_ref=source, dst_ref=target, send_sem=send, recv_sem=receive,
                device_id=device, device_id_type=MESH,
            )
            copy.wait_send() if finish else copy.start()

    def keep(finish, condition, source, target, sem):
        @pl.when(condition)
        def _():
            copy = pltpu.make_async_copy(source, target, sem)
            copy.wait() if finish else copy.start()

    def arrived(condition, target, receive):
        @pl.when(condition)
        def _():
            pltpu.make_async_remote_copy(
                src_ref=target, dst_ref=target, send_sem=receive, recv_sem=receive,
                device_id=(row, col), device_id_type=MESH,
            ).wait_recv()

    def onward(dz, dy):
        open_ways = []
        if dy == 0 and dz <= 0:
            open_ways.append(0)
        if dy == 0 and dz >= 0:
            open_ways.append(1)
        if dy <= 0:
            open_ways.append(2)
        if dy >= 0:
            open_ways.append(3)
        return open_ways

    offsets = sorted(
        ((dz, dy) for dz in range(1 - z_count, z_count) for dy in range(1 - y_count, y_count)),
        key=lambda o: (abs(o[0]) + abs(o[1]), abs(o[1])),
    )
    true = row >= 0
    leading = row < 2

    def present(dz, dy):
        inside = jnp.logical_and(z + dz >= 0, z + dz < z_count)
        inside = jnp.logical_and(inside, jnp.logical_and(y + dy >= 0, y + dy < y_count))
        slab = (z + dz) * y_count + y + dy
        return inside, jnp.where(inside, slab, 0)

    def lead_event(dz, dy, finish=False):
        inside, slab = present(dz, dy)
        mine = jnp.logical_and(inside, leading)
        half = jnp.where(leading, row, 0)
        target = leads.at[half, slab]
        first = dz == 0 and dy == 0
        if first:
            keep(finish, mine, grads.at[0, 0], target, local.at[0])
        elif not finish:
            arrived(mine, target, lead_recv.at[half, slab])
        source = grads.at[0, 0] if first else target
        for way in onward(dz, dy):
            push(finish, jnp.logical_and(mine, steps[way][0]), source, target,
                 lead_send.at[slab, way], lead_recv.at[half, slab], (row, steps[way][1]))
        for k, other in enumerate(others):
            push(finish, mine, source, target, lead_send.at[slab, 4 + k], lead_recv.at[half, slab],
                 (other, col))

    def rows_event(dz, dy, finish=False):
        inside, slab = present(dz, dy)
        target = rows.at[:, :, slab]
        first = dz == 0 and dy == 0
        if first:
            keep(finish, true, grads, target, local.at[1])
        elif not finish:
            arrived(inside, target, rows_recv.at[slab])
        source = grads if first else target
        for way in onward(dz, dy):
            push(finish, jnp.logical_and(inside, steps[way][0]), source, target,
                 rows_send.at[slab, way], rows_recv.at[slab], (row, steps[way][1]))
        forward = jnp.logical_and(inside, owner)
        picked = grads.at[:, group] if first else rows.at[:, group, slab]
        for k, other in enumerate(others):
            push(finish, forward, picked, cols.at[:, slab], cols_send.at[slab, k], cols_recv.at[slab],
                 (other, col))
        keep(finish, forward, picked, cols.at[:, slab], cols_send.at[slab, row_count - 1])

    def order_event(finish=False):
        for k, other in enumerate(others):
            push(finish, true, order, orders.at[row], order_send.at[k], order_recv.at[row],
                 (other, col))
        keep(finish, true, order, orders.at[row], local.at[2])

    lead_event(0, 0)
    order_event()
    for offset in offsets[1:]:
        lead_event(*offset)
    rows_event(0, 0)
    for half in range(2):
        for slab in range(col_count):
            arrived(row != half, leads.at[half, slab], lead_recv.at[half, slab])
    for other in others:
        arrived(true, orders.at[other], order_recv.at[other])
    for offset in offsets:
        lead_event(*offset, finish=True)
    order_event(finish=True)
    strips = corner.shape[0] // STRIP

    def meanwhile(index):
        for turn in range(strips):
            @pl.when(index == turn)
            def _():
                for offset in offsets[1:]:
                    if min(abs(offset[0]) + abs(offset[1]), strips) == turn + 1:
                        rows_event(*offset)

    corner_body(leads, orders, weights, cand_out, squares_out, lower_out, inv_high, inv_low,
                corner, upper, inverse, work, meanwhile)
    for slab in range(col_count):
        arrived(jnp.logical_not(owner), cols.at[:, slab], cols_recv.at[slab])
    for offset in offsets:
        rows_event(*offset, finish=True)


def gather_call(row_count, col_count, grads, order, weights):
    local_cols, ratio, part, features = grads.shape
    local_rows, size = order.shape
    whole = 2 * size
    hbm = pl.BlockSpec(memory_space=pl.ANY)
    vmem = pl.BlockSpec(memory_space=pltpu.VMEM)
    dma = pltpu.SemaphoreType.DMA
    return pl.pallas_call(
        functools.partial(gather_kernel, row_count, col_count),
        out_shape=(
            jax.ShapeDtypeStruct((local_cols, ratio, col_count, part, features), BF16),
            jax.ShapeDtypeStruct((local_cols, col_count, part, features), BF16),
            jax.ShapeDtypeStruct((row_count, local_rows, size), jnp.int32),
            jax.ShapeDtypeStruct((whole, features), BF16),
            jax.ShapeDtypeStruct((8, whole), F32),
            jax.ShapeDtypeStruct((whole, whole), F32),
            jax.ShapeDtypeStruct((whole, whole), BF16),
            jax.ShapeDtypeStruct((whole, whole), BF16),
        ),
        in_specs=[pl.BlockSpec(memory_space=pltpu.HBM), hbm, vmem],
        out_specs=(hbm, hbm, vmem, vmem, vmem, vmem, vmem, vmem),
        scratch_shapes=[
            pltpu.VMEM((2, col_count, part, features), BF16),
            pltpu.VMEM((whole, whole), F32),
            pltpu.VMEM((whole, whole), F32),
            pltpu.VMEM((whole, whole), F32),
            pltpu.VMEM((STRIP, 2 * STRIP), F32),
            dma((col_count, 3 + row_count)),
            dma((col_count, 4)),
            dma((col_count, row_count)),
            dma((row_count,)),
            dma((2, col_count)),
            dma((col_count,)),
            dma((col_count,)),
            dma((row_count,)),
            dma((3,)),
        ],
        compiler_params=pltpu.CompilerParams(
            collective_id=0, has_side_effects=True, vmem_limit_bytes=32 << 20
        ),
        name="gather",
    )(grads, order, weights)


def per_device(gradients, feature_weights, order):
    row_count = lax.axis_size("row")
    col_count = lax.axis_size("col")
    ratio = col_count // row_count
    local_rows, _, _, part, features = gradients.shape
    size = order.shape[2]
    weights = feature_weights.reshape(1, features)
    rows, cols, orders, *corner = gather_call(
        row_count, col_count, gradients.reshape(local_rows // ratio, ratio, part, features),
        order.reshape(local_rows, size), weights,
    )
    return window_call(
        row_count, col_count, rows.reshape(local_rows, size, features), orders,
        cols.reshape(local_rows // ratio, size, features), weights, corner,
    )


def solution(mesh):
    placed = (P(None, "row", "col", None, None), P(), P(None, "row", None))
    return jax.shard_map(
        per_device,
        mesh=mesh,
        in_specs=placed,
        out_specs=P(None, "row", None, "col", None, None),
        check_vma=False,
    )
```

```python
import functools

import jax
import jax.numpy as jnp
from jax import lax
from jax.experimental import pallas as pl
from jax.experimental.pallas import tpu as pltpu
from jax.sharding import PartitionSpec as P

RIDGE = 0.5
F32 = jnp.float32
BF16 = jnp.bfloat16


def mm(a, b):
    return jnp.dot(a, b, preferred_element_type=F32)


def mm_nt(a, b):
    return lax.dot_general(a, b, (((1,), (1,)), ((), ())), preferred_element_type=F32)


def mm_tn(a, b):
    return lax.dot_general(a, b, (((0,), (0,)), ((), ())), preferred_element_type=F32)


def split(x):
    high = x.astype(BF16)
    return high, (x - high.astype(F32)).astype(BF16)


def mm3(product, a, b):
    a_high, a_low = a
    b_high, b_low = b
    return product(a_high, b_high) + (product(a_high, b_low) + product(a_low, b_high))


def ordered(raw, order_row):
    size = raw.shape[0]
    source = lax.broadcasted_iota(jnp.int32, (size, size), 0)
    chosen = jnp.where(source == order_row, 1.0, 0.0).astype(BF16)
    return mm_tn(chosen, raw).astype(BF16)


def scale(cand, weights):
    widened = cand.astype(F32)
    scaled = (widened * weights).astype(BF16)
    return scaled, jnp.sum(scaled.astype(F32) * widened, axis=1, keepdims=True)


def as_row(column):
    size = column.shape[0]
    return jnp.transpose(jnp.broadcast_to(column, (size, 128)))[0:8, :]


def tile(scaled, squares, cand, squares_row):
    return jnp.exp(-0.5 * (squares + squares_row - 2.0 * mm_nt(scaled, cand)))


def eye(size):
    rows = lax.broadcasted_iota(jnp.int32, (size, size), 0)
    return rows == lax.broadcasted_iota(jnp.int32, (size, size), 1)


STRIP = 128
PAIR = 2
MICRO = 16


def factor_strip(work):
    sub = lax.broadcasted_iota(jnp.int32, (MICRO, 128), 0)
    for step in range(STRIP // MICRO):
        base = step * MICRO
        rows = work[base : base + MICRO, :]
        left, right = rows[:, :128], rows[:, 128:]
        lanes = [
            jnp.broadcast_to(left[:, base + j : base + j + 1], (MICRO, 128)) for j in range(MICRO)
        ]
        for k in range(MICRO):
            pivot = lax.rsqrt(jnp.broadcast_to(lanes[k][k : k + 1, :], (MICRO, 128)))
            below = jnp.where(sub > k, lanes[k], 0.0) * (pivot * pivot)
            for j in range(k + 1, MICRO):
                lanes[j] = lanes[j] - below * jnp.broadcast_to(lanes[k][j : j + 1, :], (MICRO, 128))
            left = jnp.where(
                sub == k,
                left * pivot,
                left - below * jnp.broadcast_to(left[k : k + 1], (MICRO, 128)),
            )
            right = jnp.where(
                sub == k,
                right * pivot,
                right - below * jnp.broadcast_to(right[k : k + 1], (MICRO, 128)),
            )
        done = jnp.concatenate([left, right], axis=1)
        work[base : base + MICRO, :] = done
        if base + MICRO < STRIP:
            high = done.astype(BF16).astype(F32)
            low = done - high
            rhs = jnp.concatenate([high, low, high], axis=0).astype(BF16)
            left_high, left_low = high[:, :128], low[:, :128]
            lhs = jnp.concatenate(
                [left_high, left_high, left_low, jnp.zeros((128 - 3 * MICRO, 128), F32)], axis=0
            )
            turned = jnp.transpose(lhs)[base + MICRO :, : 3 * MICRO].astype(BF16)
            work[base + MICRO :, :] = work[base + MICRO :, :] - mm(turned, rhs)


def corner_body(raw, order, weights, cand_out, squares_out, lower_out, inv_high, inv_low,
                corner, upper, inverse, work, meanwhile):
    size = raw.shape[1] * raw.shape[2]
    cands, scaleds, squares = [], [], []
    for block in range(2):
        cand = ordered(raw[block].reshape(size, raw.shape[3]), order[block, 0:1, :])
        scaled, square = scale(cand, weights[...])
        cand_out[block * size : (block + 1) * size, :] = cand
        squares_out[:, block * size : (block + 1) * size] = as_row(square)
        cands.append(cand)
        scaleds.append(scaled)
        squares.append(square)
    for block in range(2):
        own = slice(block * size, (block + 1) * size)
        square = tile(scaleds[block], squares[block], cands[block], squares_out[0:1, own])
        square = 0.5 * (square + jnp.transpose(square))
        corner[own, own] = square + jnp.where(eye(size), RIDGE, 0.0)
    cross = tile(scaleds[1], squares[1], cands[0], squares_out[0:1, :size])
    corner[:size, size:] = jnp.transpose(cross)
    corner[size:, :size] = cross
    upper[...] = jnp.zeros_like(upper)
    inverse[...] = jnp.zeros_like(inverse)

    def strip(index, _):
        meanwhile(index)
        own = pl.ds(pl.multiple_of(index * STRIP, STRIP), STRIP)
        left = split(jnp.transpose(upper[:, own]))
        current = corner[own, :] - mm3(mm, left, split(upper[...]))
        inverse_part = mm3(mm, left, split(inverse[...]))
        corner[own, :] = current
        work[:, :STRIP] = corner[own, own]
        work[:, STRIP:] = jnp.where(eye(STRIP), 1.0, 0.0)
        factor_strip(work)
        diagonal_inverse = work[:, STRIP:]
        turn = split(diagonal_inverse)
        rows = mm3(mm, turn, split(current))
        column = lax.broadcasted_iota(jnp.int32, rows.shape, 1)
        row = lax.broadcasted_iota(jnp.int32, rows.shape, 0) + index * STRIP
        upper[own, :] = jnp.where(column >= row, rows, 0.0)
        inverse[own, :] = -mm3(mm, turn, split(inverse_part))
        inverse[own, own] = diagonal_inverse
        return 0

    lax.fori_loop(0, corner.shape[0] // STRIP, strip, 0)
    lower_out[...] = jnp.transpose(upper[...])
    high, low = split(inverse[...])
    inv_high[...] = high
    inv_low[...] = low


def window_kernel(row_count, col_count, rows_raw, orders, cols_raw, weights,
                  lead, lead_squares, lower, inv_high, inv_low, out,
                  col_cand, col_squares, col_stack, inv_first, inv_second):
    step = pl.program_id(0)
    row_index, col_index = lax.axis_index("row"), lax.axis_index("col")
    ratio = col_count // row_count
    source, group = lax.rem(col_index, row_count), lax.div(col_index, row_count)
    size = rows_raw.shape[1]
    local_cols = cols_raw.shape[0]

    def solve(scaled, squares):
        entries = tile(scaled, squares, lead[...], lead_squares[0:1, :])
        high, low = split(entries)
        stacked = jnp.concatenate([high[:, :size], high[:, :size], low[:, :size]], axis=1)
        first = mm_nt(stacked, inv_first[...])
        second = mm_nt(jnp.concatenate([high, high, low], axis=1), inv_second[...])
        return jnp.concatenate([first, second], axis=1)

    def placed(solved, block):
        start = pl.multiple_of(jnp.minimum(block, 1) * size, size)
        return jnp.where(block < 2, lower[pl.ds(start, size), :], solved)

    @pl.when(step == 0)
    def _():
        top, bottom = slice(0, size), slice(size, 2 * size)
        inv_first[...] = jnp.concatenate(
            [inv_high[top, top], inv_low[top, top], inv_high[top, top]], axis=1
        )
        inv_second[...] = jnp.concatenate(
            [inv_high[bottom, :], inv_low[bottom, :], inv_high[bottom, :]], axis=1
        )
        for b in range(local_cols):
            own = slice(b * size, (b + 1) * size)
            cand = ordered(cols_raw[b], orders[source, pl.ds(b * ratio + group, 1), :])
            scaled, squares = scale(cand, weights[...])
            high, low = split(placed(solve(scaled, squares), b * col_count + col_index))
            col_cand[own, :] = cand
            col_squares[:, own] = as_row(squares)
            col_stack[own, :] = jnp.concatenate([high, low, high], axis=1)

    pair = [PAIR * step + half for half in range(PAIR)]
    cand = jnp.concatenate(
        [ordered(rows_raw[half], orders[row_index, pl.ds(at, 1), :]) for half, at in enumerate(pair)]
    )
    scaled, squares = scale(cand, weights[...])
    solved = solve(scaled, squares)
    labels = [at * row_count + row_index for at in pair]
    spans = [slice(half * size, (half + 1) * size) for half in range(PAIR)]
    factors = jnp.concatenate([placed(solved[span], label) for span, label in zip(spans, labels)])
    high, low = split(factors)
    halves = jnp.concatenate([high, high, low], axis=1)
    for b in range(local_cols):
        own = slice(b * size, (b + 1) * size)
        column = b * col_count + col_index
        both = tile(scaled, squares, col_cand[own, :], col_squares[0:1, own])
        both = both - mm_nt(halves, col_stack[own, :])
        for half, label in enumerate(labels):
            ridge = jnp.where(label == column, RIDGE, 0.0)
            entries = both[spans[half]] + jnp.where(eye(size), ridge, 0.0)
            entries = jnp.where(label < 2, 0.0, entries)
            if b == 0:
                part = factors[spans[half]]
                lead_part = jnp.where(column == 0, part[:, :size], part[:, size:])
                entries = jnp.where(column < 2, lead_part, entries)
            out[half, 0, b, 0] = entries


def window_call(row_count, col_count, rows_raw, orders, cols_raw, weights, corner):
    local_rows, size, features = rows_raw.shape
    local_cols = cols_raw.shape[0]
    whole = 2 * size

    def fixed(shape):
        return pl.BlockSpec(shape, lambda i, *_: (0,) * len(shape))

    return pl.pallas_call(
        functools.partial(window_kernel, row_count, col_count),
        out_shape=jax.ShapeDtypeStruct((local_rows, 1, local_cols, 1, size, size), F32),
        grid=(local_rows // PAIR,),
        in_specs=[
            pl.BlockSpec((PAIR, size, features), lambda i: (i, 0, 0)),
            fixed((row_count, local_rows, size)),
            fixed((local_cols, size, features)),
            fixed((1, features)),
            fixed((whole, features)),
            fixed((8, whole)),
            fixed((whole, whole)),
            fixed((whole, whole)),
            fixed((whole, whole)),
        ],
        out_specs=pl.BlockSpec(
            (PAIR, 1, local_cols, 1, size, size), lambda i: (i, 0, 0, 0, 0, 0)
        ),
        scratch_shapes=[
            pltpu.VMEM((local_cols * size, features), BF16),
            pltpu.VMEM((8, local_cols * size), F32),
            pltpu.VMEM((local_cols * size, 3 * whole), BF16),
            pltpu.VMEM((size, 3 * size), BF16),
            pltpu.VMEM((size, 3 * whole), BF16),
        ],
        compiler_params=pltpu.CompilerParams(vmem_limit_bytes=40 << 20),
        name="window",
    )(rows_raw, orders, cols_raw, weights, *corner)


MESH = pl.DeviceIdType.MESH


def gather_kernel(row_count, col_count, grads, order, weights, rows, cols, orders,
                  cand_out, squares_out, lower_out, inv_high, inv_low,
                  leads, corner, upper, inverse, work,
                  lead_send, rows_send, cols_send, order_send,
                  lead_recv, rows_recv, cols_recv, order_recv, local):
    row, col = lax.axis_index("row"), lax.axis_index("col")
    y_count = max(row_count // 2, 1)
    z_count = col_count // y_count
    z, y = lax.div(col, y_count), lax.rem(col, y_count)
    owner = row == lax.rem(col, row_count)
    group = lax.div(col, row_count)
    steps = (
        (z < z_count - 1, col + y_count),
        (z > 0, col - y_count),
        (y < y_count - 1, col + 1),
        (y > 0, col - 1),
    )
    others = [lax.rem(row + k, row_count) for k in range(1, row_count)]

    barrier = pltpu.get_barrier_semaphore()
    expected = row_count - 1
    for other in others:
        pl.semaphore_signal(barrier, inc=1, device_id=(other, col), device_id_type=MESH)
    for inside, neighbour in steps:
        @pl.when(inside)
        def _():
            pl.semaphore_signal(barrier, inc=1, device_id=(row, neighbour), device_id_type=MESH)

        expected = expected + jnp.where(inside, 1, 0)
    pl.semaphore_wait(barrier, expected)

    def push(finish, condition, source, target, send, receive, device):
        @pl.when(condition)
        def _():
            copy = pltpu.make_async_remote_copy(
                src_ref=source, dst_ref=target, send_sem=send, recv_sem=receive,
                device_id=device, device_id_type=MESH,
            )
            copy.wait_send() if finish else copy.start()

    def keep(finish, condition, source, target, sem):
        @pl.when(condition)
        def _():
            copy = pltpu.make_async_copy(source, target, sem)
            copy.wait() if finish else copy.start()

    def arrived(condition, target, receive):
        @pl.when(condition)
        def _():
            pltpu.make_async_remote_copy(
                src_ref=target, dst_ref=target, send_sem=receive, recv_sem=receive,
                device_id=(row, col), device_id_type=MESH,
            ).wait_recv()

    def onward(dz, dy):
        open_ways = []
        if dy == 0 and dz <= 0:
            open_ways.append(0)
        if dy == 0 and dz >= 0:
            open_ways.append(1)
        if dy <= 0:
            open_ways.append(2)
        if dy >= 0:
            open_ways.append(3)
        return open_ways

    offsets = sorted(
        ((dz, dy) for dz in range(1 - z_count, z_count) for dy in range(1 - y_count, y_count)),
        key=lambda o: (abs(o[0]) + abs(o[1]), abs(o[1])),
    )
    true = row >= 0
    leading = row < 2

    def present(dz, dy):
        inside = jnp.logical_and(z + dz >= 0, z + dz < z_count)
        inside = jnp.logical_and(inside, jnp.logical_and(y + dy >= 0, y + dy < y_count))
        slab = (z + dz) * y_count + y + dy
        return inside, jnp.where(inside, slab, 0)

    def lead_event(dz, dy, finish=False):
        inside, slab = present(dz, dy)
        mine = jnp.logical_and(inside, leading)
        half = jnp.where(leading, row, 0)
        target = leads.at[half, slab]
        first = dz == 0 and dy == 0
        if first:
            keep(finish, mine, grads.at[0, 0], target, local.at[0])
        elif not finish:
            arrived(mine, target, lead_recv.at[half, slab])
        source = grads.at[0, 0] if first else target
        for way in onward(dz, dy):
            push(finish, jnp.logical_and(mine, steps[way][0]), source, target,
                 lead_send.at[slab, way], lead_recv.at[half, slab], (row, steps[way][1]))
        for k, other in enumerate(others):
            push(finish, mine, source, target, lead_send.at[slab, 4 + k], lead_recv.at[half, slab],
                 (other, col))

    def rows_event(dz, dy, finish=False):
        inside, slab = present(dz, dy)
        target = rows.at[:, :, slab]
        first = dz == 0 and dy == 0
        if first:
            keep(finish, true, grads, target, local.at[1])
        elif not finish:
            arrived(inside, target, rows_recv.at[slab])
        source = grads if first else target
        for way in onward(dz, dy):
            push(finish, jnp.logical_and(inside, steps[way][0]), source, target,
                 rows_send.at[slab, way], rows_recv.at[slab], (row, steps[way][1]))
        forward = jnp.logical_and(inside, owner)
        picked = grads.at[:, group] if first else rows.at[:, group, slab]
        for k, other in enumerate(others):
            push(finish, forward, picked, cols.at[:, slab], cols_send.at[slab, k], cols_recv.at[slab],
                 (other, col))
        keep(finish, forward, picked, cols.at[:, slab], cols_send.at[slab, row_count - 1])

    def order_event(finish=False):
        for k, other in enumerate(others):
            push(finish, true, order, orders.at[row], order_send.at[k], order_recv.at[row],
                 (other, col))
        keep(finish, true, order, orders.at[row], local.at[2])

    lead_event(0, 0)
    order_event()
    for offset in offsets[1:]:
        lead_event(*offset)
    rows_event(0, 0)
    for half in range(2):
        for slab in range(col_count):
            arrived(row != half, leads.at[half, slab], lead_recv.at[half, slab])
    for other in others:
        arrived(true, orders.at[other], order_recv.at[other])
    for offset in offsets:
        lead_event(*offset, finish=True)
    order_event(finish=True)
    strips = corner.shape[0] // STRIP

    def meanwhile(index):
        for turn in range(strips):
            @pl.when(index == turn)
            def _():
                for offset in offsets[1:]:
                    if min(abs(offset[0]) + abs(offset[1]), strips) == turn + 1:
                        rows_event(*offset)

    corner_body(leads, orders, weights, cand_out, squares_out, lower_out, inv_high, inv_low,
                corner, upper, inverse, work, meanwhile)
    for slab in range(col_count):
        arrived(jnp.logical_not(owner), cols.at[:, slab], cols_recv.at[slab])
    for offset in offsets:
        rows_event(*offset, finish=True)


def gather_call(row_count, col_count, grads, order, weights):
    local_cols, ratio, part, features = grads.shape
    local_rows, size = order.shape
    whole = 2 * size
    hbm = pl.BlockSpec(memory_space=pl.ANY)
    vmem = pl.BlockSpec(memory_space=pltpu.VMEM)
    dma = pltpu.SemaphoreType.DMA
    return pl.pallas_call(
        functools.partial(gather_kernel, row_count, col_count),
        out_shape=(
            jax.ShapeDtypeStruct((local_cols, ratio, col_count, part, features), BF16),
            jax.ShapeDtypeStruct((local_cols, col_count, part, features), BF16),
            jax.ShapeDtypeStruct((row_count, local_rows, size), jnp.int32),
            jax.ShapeDtypeStruct((whole, features), BF16),
            jax.ShapeDtypeStruct((8, whole), F32),
            jax.ShapeDtypeStruct((whole, whole), F32),
            jax.ShapeDtypeStruct((whole, whole), BF16),
            jax.ShapeDtypeStruct((whole, whole), BF16),
        ),
        in_specs=[pl.BlockSpec(memory_space=pltpu.HBM), hbm, vmem],
        out_specs=(hbm, hbm, vmem, vmem, vmem, vmem, vmem, vmem),
        scratch_shapes=[
            pltpu.VMEM((2, col_count, part, features), BF16),
            pltpu.VMEM((whole, whole), F32),
            pltpu.VMEM((whole, whole), F32),
            pltpu.VMEM((whole, whole), F32),
            pltpu.VMEM((STRIP, 2 * STRIP), F32),
            dma((col_count, 3 + row_count)),
            dma((col_count, 4)),
            dma((col_count, row_count)),
            dma((row_count,)),
            dma((2, col_count)),
            dma((col_count,)),
            dma((col_count,)),
            dma((row_count,)),
            dma((3,)),
        ],
        compiler_params=pltpu.CompilerParams(
            collective_id=0, has_side_effects=True, vmem_limit_bytes=32 << 20
        ),
        name="gather",
    )(grads, order, weights)


def per_device(gradients, feature_weights, order):
    row_count = lax.axis_size("row")
    col_count = lax.axis_size("col")
    ratio = col_count // row_count
    local_rows, _, _, part, features = gradients.shape
    size = order.shape[2]
    weights = feature_weights.reshape(1, features)
    rows, cols, orders, *corner = gather_call(
        row_count, col_count, gradients.reshape(local_rows // ratio, ratio, part, features),
        order.reshape(local_rows, size), weights,
    )
    return window_call(
        row_count, col_count, rows.reshape(local_rows, size, features), orders,
        cols.reshape(local_rows // ratio, size, features), weights, corner,
    )


def solution(mesh):
    placed = (P(None, "row", "col", None, None), P(), P(None, "row", None))
    return jax.shard_map(
        per_device,
        mesh=mesh,
        in_specs=placed,
        out_specs=P(None, "row", None, "col", None, None),
        check_vma=False,
    )
```
